256 devices in a mesh: tm: 16 (over y, z_hi, core), height: 16 (over x, z_lo).
Axes of the slice: x: 4, y: 4, z: 8 (z_hi: 2, z_lo: 4; z = z_hi * 4 + z_lo), core: 2. Of those that a mesh axis runs over, the one named last changes fastest.
Arguments:
- latent: bfloat16 [32, 32, 80, 3072], P('tm', 'height'), may hold values from -6 to 6
- mod_shift: float32 [3072], replicated, may hold values from -3 to 3
- mod_scale: float32 [3072], replicated, may hold values from -0.5 to 4
- w_qkv: bfloat16 [3072, 4608], P('height'), may hold values from -0.3247595 to 0.3247595
- extents: int32 [12, 3], replicated, may hold values from 0 to 3, as said below
Outputs:
- attended: bfloat16 [32, 32, 80, 1536], P('tm', 'height')
The draws below stay inside these ranges and needn't reach their ends.
Inputs may be any that keep to these rules, and one draw needn't show every extreme that they name: `extents`: extents along frames and rows lie in 0 to 1, along columns in 0 to 3; each of the three largest values is taken by some head.
All inputs are finite; a program needn't handle non-finite values.
Results may differ from the reference program's by a relative error of at most 0.003.
The reference program's roundings to bfloat16 on the way (of `modulated`, `qkv` and `weights`) count: a program that leaves them out, or rounds other values in their place, can miss the bound.
Values may be sent and summed in bfloat16 or wider, within the bound.
A program may use at most 128 MiB of HBM per device.

```python
import jax
import jax.numpy as jnp
from jax import lax

D = 3072
HW = 12
HD = 128
COLS = 80
TILE_W = 8
EXT = 1
EXT_W = 3
FRAMES = 32
ROWS = 32


def draw_latent(key, part):
    drawn_draw = jax.random.normal(key, (FRAMES, ROWS, COLS, D), jnp.float32)
    return jnp.clip(drawn_draw, -6.0, 6.0).astype(jnp.bfloat16)


def draw_w_qkv(key, part):
    spread_factor = 1.0 / D ** 0.5
    drawn_draw = jax.random.normal(key, (D, 3 * HW * HD), jnp.float32)
    return (jnp.clip(drawn_draw, -6.0, 6.0) * spread_factor).astype(jnp.bfloat16)


def draw_mod_scale(key, part):
    return jax.random.uniform(key, (D,), jnp.float32, -0.5, 1.5)


def draw_extents(key, part):
    first = jax.random.fold_in(key, 11)
    second = jax.random.fold_in(key, 23)
    limits = jnp.array([EXT, EXT, EXT_W], dtype=jnp.int32)
    raw = jax.random.randint(first, (HW, 3), 0, 1 << 20, dtype=jnp.int32)
    picked = raw % (limits[None, :] + 1)
    heads = jax.random.randint(second, (3,), 0, HW, dtype=jnp.int32)
    rows_here = jnp.arange(HW, dtype=jnp.int32)[:, None] == heads[None, :]
    return jnp.where(rows_here, limits[None, :], picked).astype(jnp.int32)


def scatter_about(own_key, dims, width, bound, held_as=jnp.bfloat16):
    result = jax.random.normal(own_key, dims, jnp.float32) * width
    return jnp.minimum(jnp.maximum(result, -bound), bound).astype(held_as)


def setup_inputs(seed: int = 0) -> dict:
    arg_keys = jax.random.split(jax.random.key(seed), 6)
    return {
        "latent": draw_latent(jax.random.fold_in(arg_keys[5], 71), 0),
        "mod_shift": scatter_about(arg_keys[1], (D,), 0.5, 3.0, jnp.float32),
        "mod_scale": draw_mod_scale(jax.random.fold_in(arg_keys[5], 71), 0),
        "w_qkv": draw_w_qkv(jax.random.fold_in(arg_keys[5], 71), 0),
        "extents": draw_extents(jax.random.fold_in(arg_keys[5], 71), 0),
    }


def reference(latent, mod_shift, mod_scale, w_qkv, extents):
    feats = latent.astype(jnp.float32)
    mean = lax.optimization_barrier(jnp.mean(feats, axis=-1, keepdims=True))
    var = lax.optimization_barrier(jnp.mean((feats - mean) ** 2, axis=-1, keepdims=True))
    normed = (feats - mean) * lax.rsqrt(var + 1e-06)
    modulated = (normed * (1.0 + mod_scale) + mod_shift).astype(jnp.bfloat16)
    flat = modulated.reshape(-1, D)
    qkv = jnp.dot(flat, w_qkv, preferred_element_type=jnp.float32).astype(jnp.bfloat16)
    qkv = qkv.reshape(FRAMES, ROWS, COLS, 3, HW, HD)
    query = qkv[:, :, :, 0]
    keys = jnp.pad(qkv[:, :, :, 1], ((1, 1), (1, 1), (0, 0), (0, 0), (0, 0)))
    values = jnp.pad(qkv[:, :, :, 2], ((1, 1), (1, 1), (0, 0), (0, 0), (0, 0)))
    inv = 1.0 / HD ** 0.5
    span = 9 * COLS
    kidx = jnp.arange(span, dtype=jnp.int32)
    dframe = kidx // (3 * COLS) - 1
    drow = kidx // COLS % 3 - 1
    kcol = kidx % COLS
    qcol = jnp.arange(COLS, dtype=jnp.int32)
    coldist = jnp.abs(qcol[:, None] // TILE_W - kcol[None, :] // TILE_W)
    zero = jnp.int32(0)

    def one_line(index):
        frame = index // ROWS
        row = index % ROWS
        qline = query[frame, row].astype(jnp.float32)
        kwin = lax.dynamic_slice(keys, (frame, row, zero, zero, zero), (3, 3, COLS, HW, HD)).reshape(span, HW, HD)
        vwin = lax.dynamic_slice(values, (frame, row, zero, zero, zero), (3, 3, COLS, HW, HD)).reshape(span, HW, HD)
        scores = jnp.einsum('qhd,khd->hqk', qline, kwin.astype(jnp.float32)) * inv
        gframe = frame + dframe
        grow = row + drow
        valid = (gframe >= 0) & (gframe < FRAMES) & (grow >= 0) & (grow < ROWS)
        allowed = valid[None, None, :] & (jnp.abs(dframe)[None, None, :] <= extents[:, 0][:, None, None])
        allowed = allowed & (jnp.abs(drow)[None, None, :] <= extents[:, 1][:, None, None])
        allowed = allowed & (coldist[None, :, :] <= extents[:, 2][:, None, None])
        masked = jnp.where(allowed, scores, -1e+30)
        top = lax.optimization_barrier(jnp.max(masked, axis=-1, keepdims=True))
        expo = jnp.where(allowed, jnp.exp(masked - top), 0.0)
        weights = (expo / lax.optimization_barrier(jnp.sum(expo, axis=-1, keepdims=True))).astype(jnp.bfloat16)
        out = jnp.einsum('hqk,khd->qhd', weights.astype(jnp.float32), vwin.astype(jnp.float32))
        return out.astype(jnp.bfloat16).reshape(COLS, HW * HD)
    lines = lax.map(one_line, jnp.arange(FRAMES * ROWS, dtype=jnp.int32))
    return lines.reshape(FRAMES, ROWS, COLS, HW * HD)
```

```python
import numpy as np
import jax
import jax.numpy as jnp
from jax import lax
from jax.sharding import Mesh, PartitionSpec as P

HW = 12
HD = 128
TILE_W = 8

TM = ("tp", "c")
HT = ("hx", "hz")


def on_device(latent, mod_shift, mod_scale, w_qkv, extents):
    fd, rd, ncols, dim = latent.shape
    nt = lax.axis_size("tp") * 2
    nh = lax.axis_size("hx") * lax.axis_size("hz")
    hh = HW // 2
    hw = hh * HD
    width = HW * HD
    c = lax.axis_index("c")
    tp = lax.axis_index("tp")
    h = lax.axis_index("hx") * lax.axis_size("hz") + lax.axis_index("hz")
    first_core = c == 0

    feats = latent.astype(jnp.float32)
    mean = jnp.mean(feats, axis=-1, keepdims=True)
    var = jnp.mean((feats - mean) ** 2, axis=-1, keepdims=True)
    normed = (feats - mean) * lax.rsqrt(var + 1e-06)
    mod = (normed * (1.0 + mod_scale) + mod_shift).astype(jnp.bfloat16)

    swap = [(i, i ^ 1) for i in range(nt)]
    partner = lax.ppermute(mod, TM, swap)
    edge = jnp.where(first_core, mod[0:1], mod[fd - 1 : fd])
    p1, p2 = [], []
    for k in range(nt // 2):
        if 2 * k - 1 >= 0:
            p1.append((2 * k - 1, 2 * k))
            p2.append((2 * k - 1, 2 * k + 1))
        if 2 * k + 2 < nt:
            p1.append((2 * k + 2, 2 * k + 1))
            p2.append((2 * k + 2, 2 * k))
    recv1 = lax.ppermute(edge, TM, p1)
    recv2 = lax.ppermute(edge, TM, p2)
    chipf = jnp.concatenate(
        [
            jnp.where(first_core, recv1, recv2),
            jnp.where(first_core, mod, partner),
            jnp.where(first_core, partner, mod),
            jnp.where(first_core, recv2, recv1),
        ],
        axis=0,
    )
    up = [(i, i + 1) for i in range(nh - 1)]
    down = [(i + 1, i) for i in range(nh - 1)]
    before = lax.ppermute(chipf[:, rd - 1 : rd], HT, up)
    after = lax.ppermute(chipf[:, 0:1], HT, down)
    padded = jnp.concatenate([before, chipf, after], axis=1)
    nf, nr = 2 * fd + 2, rd + 2

    wsel = jnp.concatenate(
        [lax.dynamic_slice_in_dim(w_qkv, j * width + c * hw, hw, axis=1) for j in range(3)],
        axis=1,
    )
    wg = lax.all_gather(wsel, "hz", axis=0, tiled=True)
    wg = lax.all_gather(wg, "hx", axis=0, tiled=True)

    qtok = padded[1 : nf - 1, 1 : nr - 1].reshape(-1, dim)
    query = jnp.dot(qtok, wg[:, :hw], preferred_element_type=jnp.float32).astype(jnp.bfloat16)
    kv = jnp.dot(padded.reshape(-1, dim), wg[:, hw:], preferred_element_type=jnp.float32).astype(
        jnp.bfloat16
    )
    keys = kv[:, :hw].reshape(nf, nr, ncols, hh, HD)
    values = kv[:, hw:].reshape(nf, nr, ncols, hh, HD)
    nq = 2 * fd
    kwin = jnp.stack(
        [keys[f : f + 3, r : r + 3].reshape(9 * ncols, hh, HD) for f in range(nq) for r in range(rd)]
    )
    vwin = jnp.stack(
        [values[f : f + 3, r : r + 3].reshape(9 * ncols, hh, HD) for f in range(nq) for r in range(rd)]
    )
    qline = query.reshape(nq * rd, ncols, hh, HD)

    span = 9 * ncols
    kidx = jnp.arange(span, dtype=jnp.int32)
    dframe = kidx // (3 * ncols) - 1
    drow = kidx // ncols % 3 - 1
    kcol = kidx % ncols
    qcol = jnp.arange(ncols, dtype=jnp.int32)
    coldist = jnp.abs(qcol[:, None] // TILE_W - kcol[None, :] // TILE_W)
    line = jnp.arange(nq * rd, dtype=jnp.int32)
    gframe = tp * nq + line // rd
    grow = h * rd + line % rd
    kf = gframe[:, None] + dframe[None, :]
    kr = grow[:, None] + drow[None, :]
    valid = (kf >= 0) & (kf < nt * fd) & (kr >= 0) & (kr < nh * rd)
    ext = lax.dynamic_slice_in_dim(extents, c * hh, hh, axis=0)
    allowed = valid[:, None, None, :] & (jnp.abs(dframe)[None, None, None, :] <= ext[None, :, 0, None, None])
    allowed = allowed & (jnp.abs(drow)[None, None, None, :] <= ext[None, :, 1, None, None])
    allowed = allowed & (coldist[None, None, :, :] <= ext[None, :, 2, None, None])

    inv = 1.0 / HD**0.5
    scores = jnp.einsum("nqhd,nkhd->nhqk", qline, kwin, preferred_element_type=jnp.float32) * inv
    masked = jnp.where(allowed, scores, -1e30)
    top = jnp.max(masked, axis=-1, keepdims=True)
    expo = jnp.where(allowed, jnp.exp(masked - top), 0.0)
    weights = (expo / jnp.sum(expo, axis=-1, keepdims=True)).astype(jnp.bfloat16)
    out = jnp.einsum("nhqk,nkhd->nqhd", weights, vwin, preferred_element_type=jnp.float32)
    out = out.astype(jnp.bfloat16).reshape(nq, rd, ncols, hw)

    mine = lax.dynamic_slice_in_dim(out, c * fd, fd, axis=0)
    theirs = lax.dynamic_slice_in_dim(out, (1 - c) * fd, fd, axis=0)
    got = lax.ppermute(theirs, TM, swap)
    return jnp.where(
        first_core,
        jnp.concatenate([mine, got], axis=-1),
        jnp.concatenate([got, mine], axis=-1),
    )


def solution(mesh):
    nt, nh = mesh.shape["tm"], mesh.shape["height"]
    devs = np.asarray(mesh.devices).reshape(nt // 2, 2, nh // 4, 4)
    m = Mesh(devs, ("tp", "c", "hx", "hz"))
    in_specs = (P(TM, HT, None, None), P(), P(), P(HT, None), P())
    out_specs = P(TM, HT, None, None)
    return jax.shard_map(on_device, mesh=m, in_specs=in_specs, out_specs=out_specs, check_vma=False)
```

```python
import numpy as np
import jax
import jax.numpy as jnp
from jax import lax
from jax.sharding import Mesh, PartitionSpec as P


HW = 12
HD = 128
TILE_W = 8
NCHUNK = 2

TM = ("tp", "c")
HT = ("hx", "hz")


def on_device(latent, mod_shift, mod_scale, w_qkv, extents):
    fd, rd, ncols, dim = latent.shape
    nt = lax.axis_size("tp") * 2
    nh = lax.axis_size("hx") * lax.axis_size("hz")
    hh = HW // 2
    width = HW * HD
    c = lax.axis_index("c")
    tp = lax.axis_index("tp")
    h = lax.axis_index("hx") * lax.axis_size("hz") + lax.axis_index("hz")
    first_core = c == 0

    feats = latent.astype(jnp.float32)
    mean = jnp.mean(feats, axis=-1, keepdims=True)
    var = jnp.mean((feats - mean) ** 2, axis=-1, keepdims=True)
    normed = (feats - mean) * lax.rsqrt(var + 1e-06)
    mod = (normed * (1.0 + mod_scale) + mod_shift).astype(jnp.bfloat16)

    up = [(i, i + 1) for i in range(nh - 1)]
    down = [(i + 1, i) for i in range(nh - 1)]
    w_qkv, mod = lax.optimization_barrier((w_qkv, mod))
    before = lax.ppermute(mod[:, rd - 1 : rd], HT, up)
    after = lax.ppermute(mod[:, 0:1], HT, down)
    rowpad = jnp.concatenate([before, mod, after], axis=1)
    swap = [(i, i ^ 1) for i in range(nt)]
    partner = lax.ppermute(rowpad, TM, swap)
    edge = jnp.where(first_core, rowpad[0:1], rowpad[fd - 1 : fd])
    p1, p2 = [], []
    for k in range(nt // 2):
        if 2 * k - 1 >= 0:
            p1.append((2 * k - 1, 2 * k))
            p2.append((2 * k - 1, 2 * k + 1))
        if 2 * k + 2 < nt:
            p1.append((2 * k + 2, 2 * k + 1))
            p2.append((2 * k + 2, 2 * k))
    recv1 = lax.ppermute(edge, TM, p1)
    recv2 = lax.ppermute(edge, TM, p2)
    padded = jnp.concatenate(
        [
            jnp.where(first_core, recv1, recv2),
            jnp.where(first_core, rowpad, partner),
            jnp.where(first_core, partner, rowpad),
            jnp.where(first_core, recv2, recv1),
        ],
        axis=0,
    )
    nf, nr = 2 * fd + 2, rd + 2
    nq = 2 * fd
    qtok = padded[1 : nf - 1, 1 : nr - 1].reshape(-1, dim)
    ptok = padded.reshape(-1, dim)

    span = 9 * ncols
    kidx = jnp.arange(span, dtype=jnp.int32)
    dframe = kidx // (3 * ncols) - 1
    drow = kidx // ncols % 3 - 1
    kcol = kidx % ncols
    qcol = jnp.arange(ncols, dtype=jnp.int32)
    coldist = jnp.abs(qcol[:, None] // TILE_W - kcol[None, :] // TILE_W)
    line = jnp.arange(nq * rd, dtype=jnp.int32)
    gframe = tp * nq + line // rd
    grow = h * rd + line % rd
    kf = gframe[:, None] + dframe[None, :]
    kr = grow[:, None] + drow[None, :]
    valid = (kf >= 0) & (kf < nt * fd) & (kr >= 0) & (kr < nh * rd)
    inv = 1.0 / HD**0.5

    nc = NCHUNK
    hc = hh // nc
    cw = hc * HD

    def attend(wg, head0):
        query = jnp.dot(qtok, wg[:, :cw], preferred_element_type=jnp.float32).astype(jnp.bfloat16)
        kv = jnp.dot(ptok, wg[:, cw:], preferred_element_type=jnp.float32).astype(jnp.bfloat16)
        keys = kv[:, :cw].reshape(nf, nr, ncols, hc, HD)
        values = kv[:, cw:].reshape(nf, nr, ncols, hc, HD)
        kwin = jnp.stack(
            [keys[f : f + 3, r : r + 3].reshape(span, hc, HD) for f in range(nq) for r in range(rd)]
        )
        vwin = jnp.stack(
            [values[f : f + 3, r : r + 3].reshape(span, hc, HD) for f in range(nq) for r in range(rd)]
        )
        qline = query.reshape(nq * rd, ncols, hc, HD)
        ext = lax.dynamic_slice_in_dim(extents, head0, hc, axis=0)
        allowed = valid[:, None, None, :] & (jnp.abs(dframe)[None, None, None, :] <= ext[None, :, 0, None, None])
        allowed = allowed & (jnp.abs(drow)[None, None, None, :] <= ext[None, :, 1, None, None])
        allowed = allowed & (coldist[None, None, :, :] <= ext[None, :, 2, None, None])
        scores = jnp.einsum("nqhd,nkhd->nhqk", qline, kwin, preferred_element_type=jnp.float32) * inv
        masked = jnp.where(allowed, scores, -1e30)
        top = jnp.max(masked, axis=-1, keepdims=True)
        expo = jnp.where(allowed, jnp.exp(masked - top), 0.0)
        weights = (expo / jnp.sum(expo, axis=-1, keepdims=True)).astype(jnp.bfloat16)
        out = jnp.einsum("nhqk,nkhd->nqhd", weights, vwin, preferred_element_type=jnp.float32)
        out = out.astype(jnp.bfloat16).reshape(nq, rd, ncols, cw)
        mine = lax.dynamic_slice_in_dim(out, c * fd, fd, axis=0)
        theirs = lax.dynamic_slice_in_dim(out, (1 - c) * fd, fd, axis=0)
        return mine, lax.ppermute(theirs, TM, swap)

    outs = []
    for j in range(nc):
        head0 = c * hh + j * hc
        wsel = jnp.concatenate(
            [lax.dynamic_slice_in_dim(w_qkv, part * width + head0 * HD, cw, axis=1) for part in range(3)],
            axis=1,
        )
        wg = lax.all_gather(wsel, "hz", axis=0, tiled=True)
        wg = lax.all_gather(wg, "hx", axis=0, tiled=True)
        outs.append(attend(wg, head0))
    mine = jnp.concatenate([o[0] for o in outs], axis=-1)
    got = jnp.concatenate([o[1] for o in outs], axis=-1)
    return jnp.where(
        first_core,
        jnp.concatenate([mine, got], axis=-1),
        jnp.concatenate([got, mine], axis=-1),
    )


def solution(mesh):
    nt, nh = mesh.shape["tm"], mesh.shape["height"]
    devs = np.asarray(mesh.devices).reshape(nt // 2, 2, nh // 4, 4)
    m = Mesh(devs, ("tp", "c", "hx", "hz"))
    in_specs = (P(TM, HT, None, None), P(), P(), P(HT, None), P())
    out_specs = P(TM, HT, None, None)
    return jax.shard_map(on_device, mesh=m, in_specs=in_specs, out_specs=out_specs, check_vma=False)
```

```python
import numpy as np
import jax
import jax.numpy as jnp
from jax import lax
from jax.sharding import Mesh, PartitionSpec as P


HW = 12
HD = 128
TILE_W = 8
NCHUNK = 2

TM = ("tp", "c")
HT = ("hx", "hz")


def on_device(latent, mod_shift, mod_scale, w_qkv, extents):
    fd, rd, ncols, dim = latent.shape
    nt = lax.axis_size("tp") * 2
    nh = lax.axis_size("hx") * lax.axis_size("hz")
    hh = HW // 2
    width = HW * HD
    c = lax.axis_index("c")
    tp = lax.axis_index("tp")
    h = lax.axis_index("hx") * lax.axis_size("hz") + lax.axis_index("hz")
    first_core = c == 0

    feats = latent.astype(jnp.float32)
    mean = jnp.mean(feats, axis=-1, keepdims=True)
    var = jnp.mean((feats - mean) ** 2, axis=-1, keepdims=True)
    normed = (feats - mean) * lax.rsqrt(var + 1e-06)
    mod = (normed * (1.0 + mod_scale) + mod_shift).astype(jnp.bfloat16)

    up = [(i, i + 1) for i in range(nh - 1)]
    down = [(i + 1, i) for i in range(nh - 1)]
    w_qkv, mod = lax.optimization_barrier((w_qkv, mod))
    before = lax.ppermute(mod[:, rd - 1 : rd], HT, up)
    after = lax.ppermute(mod[:, 0:1], HT, down)
    rowpad = jnp.concatenate([before, mod, after], axis=1)
    swap = [(i, i ^ 1) for i in range(nt)]
    partner = lax.ppermute(rowpad, TM, swap)
    edge = jnp.where(first_core, rowpad[0:1], rowpad[fd - 1 : fd])
    p1 = []
    for k in range(nt // 2):
        if 2 * k - 1 >= 0:
            p1.append((2 * k - 1, 2 * k))
        if 2 * k + 2 < nt:
            p1.append((2 * k + 2, 2 * k + 1))
    recv = lax.ppermute(edge, TM, p1)
    precv = lax.ppermute(recv, TM, swap)
    padded = jnp.concatenate(
        [
            jnp.where(first_core, recv, precv),
            jnp.where(first_core, rowpad, partner),
            jnp.where(first_core, partner, rowpad),
            jnp.where(first_core, precv, recv),
        ],
        axis=0,
    )
    nf, nr = 2 * fd + 2, rd + 2
    nq = 2 * fd
    qtok = padded[1 : nf - 1, 1 : nr - 1].reshape(-1, dim)
    ptok = padded.reshape(-1, dim)

    span = 9 * ncols
    kidx = jnp.arange(span, dtype=jnp.int32)
    dframe = kidx // (3 * ncols) - 1
    drow = kidx // ncols % 3 - 1
    kcol = kidx % ncols
    qcol = jnp.arange(ncols, dtype=jnp.int32)
    coldist = jnp.abs(qcol[:, None] // TILE_W - kcol[None, :] // TILE_W)
    line = jnp.arange(nq * rd, dtype=jnp.int32)
    gframe = tp * nq + line // rd
    grow = h * rd + line % rd
    kf = gframe[:, None] + dframe[None, :]
    kr = grow[:, None] + drow[None, :]
    valid = (kf >= 0) & (kf < nt * fd) & (kr >= 0) & (kr < nh * rd)
    inv = 1.0 / HD**0.5

    nc = NCHUNK
    hc = hh // nc
    cw = hc * HD

    def attend(wg, head0):
        query = jnp.dot(qtok, wg[:, :cw], preferred_element_type=jnp.float32).astype(jnp.bfloat16)
        kv = jnp.dot(ptok, wg[:, cw:], preferred_element_type=jnp.float32).astype(jnp.bfloat16)
        keys = kv[:, :cw].reshape(nf, nr, ncols, hc, HD)
        values = kv[:, cw:].reshape(nf, nr, ncols, hc, HD)
        kwin = jnp.stack(
            [keys[f : f + 3, r : r + 3].reshape(span, hc, HD) for f in range(nq) for r in range(rd)]
        )
        vwin = jnp.stack(
            [values[f : f + 3, r : r + 3].reshape(span, hc, HD) for f in range(nq) for r in range(rd)]
        )
        qline = query.reshape(nq * rd, ncols, hc, HD)
        ext = lax.dynamic_slice_in_dim(extents, head0, hc, axis=0)
        allowed = valid[:, None, None, :] & (jnp.abs(dframe)[None, None, None, :] <= ext[None, :, 0, None, None])
        allowed = allowed & (jnp.abs(drow)[None, None, None, :] <= ext[None, :, 1, None, None])
        allowed = allowed & (coldist[None, None, :, :] <= ext[None, :, 2, None, None])
        scores = jnp.einsum("nqhd,nkhd->nhqk", qline, kwin, preferred_element_type=jnp.float32) * inv
        masked = jnp.where(allowed, scores, -1e30)
        top = jnp.max(masked, axis=-1, keepdims=True)
        expo = jnp.where(allowed, jnp.exp(masked - top), 0.0)
        weights = (expo / jnp.sum(expo, axis=-1, keepdims=True)).astype(jnp.bfloat16)
        out = jnp.einsum("nhqk,nkhd->nqhd", weights, vwin, preferred_element_type=jnp.float32)
        out = out.astype(jnp.bfloat16).reshape(nq, rd, ncols, cw)
        mine = lax.dynamic_slice_in_dim(out, c * fd, fd, axis=0)
        theirs = lax.dynamic_slice_in_dim(out, (1 - c) * fd, fd, axis=0)
        return mine, lax.ppermute(theirs, TM, swap)

    outs = []
    for j in range(nc):
        head0 = c * hh + j * hc
        wsel = jnp.concatenate(
            [lax.dynamic_slice_in_dim(w_qkv, part * width + head0 * HD, cw, axis=1) for part in range(3)],
            axis=1,
        )
        wg = lax.all_gather(wsel, "hz", axis=0, tiled=True)
        wg = lax.all_gather(wg, "hx", axis=0, tiled=True)
        outs.append(attend(wg, head0))
    mine = jnp.concatenate([o[0] for o in outs], axis=-1)
    got = jnp.concatenate([o[1] for o in outs], axis=-1)
    return jnp.where(
        first_core,
        jnp.concatenate([mine, got], axis=-1),
        jnp.concatenate([got, mine], axis=-1),
    )


def solution(mesh):
    nt, nh = mesh.shape["tm"], mesh.shape["height"]
    devs = np.asarray(mesh.devices).reshape(nt // 2, 2, nh // 4, 4)
    m = Mesh(devs, ("tp", "c", "hx", "hz"))
    in_specs = (P(TM, HT, None, None), P(), P(), P(HT, None), P())
    out_specs = P(TM, HT, None, None)
    return jax.shard_map(on_device, mesh=m, in_specs=in_specs, out_specs=out_specs, check_vma=False)
```

```python
import numpy as np
import jax
import jax.numpy as jnp
from jax import lax
from jax.sharding import Mesh, PartitionSpec as P


HW = 12
HD = 128
TILE_W = 8
CHUNKS = (4, 2)

TM = ("tp", "c")
HT = ("hx", "hz")


def on_device(latent, mod_shift, mod_scale, w_qkv, extents):
    fd, rd, ncols, dim = latent.shape
    nt = lax.axis_size("tp") * 2
    nh = lax.axis_size("hx") * lax.axis_size("hz")
    hh = HW // 2
    hw = hh * HD
    width = HW * HD
    c = lax.axis_index("c")
    tp = lax.axis_index("tp")
    h = lax.axis_index("hx") * lax.axis_size("hz") + lax.axis_index("hz")
    first_core = c == 0

    feats = latent.astype(jnp.float32)
    mean = jnp.mean(feats, axis=-1, keepdims=True)
    var = jnp.mean((feats - mean) ** 2, axis=-1, keepdims=True)
    normed = (feats - mean) * lax.rsqrt(var + 1e-06)
    mod = (normed * (1.0 + mod_scale) + mod_shift).astype(jnp.bfloat16)

    up = [(i, i + 1) for i in range(nh - 1)]
    down = [(i + 1, i) for i in range(nh - 1)]
    w_qkv, mod = lax.optimization_barrier((w_qkv, mod))
    before = lax.ppermute(mod[:, rd - 1 : rd], HT, up)
    after = lax.ppermute(mod[:, 0:1], HT, down)
    rowpad = jnp.concatenate([before, mod, after], axis=1)
    swap = [(i, i ^ 1) for i in range(nt)]
    partner = lax.ppermute(rowpad, TM, swap)
    edge = jnp.where(first_core, rowpad[0:1], rowpad[fd - 1 : fd])
    p1 = []
    for k in range(nt // 2):
        if 2 * k - 1 >= 0:
            p1.append((2 * k - 1, 2 * k))
        if 2 * k + 2 < nt:
            p1.append((2 * k + 2, 2 * k + 1))
    recv = lax.ppermute(edge, TM, p1)
    precv = lax.ppermute(recv, TM, swap)
    padded = jnp.concatenate(
        [
            jnp.where(first_core, recv, precv),
            jnp.where(first_core, rowpad, partner),
            jnp.where(first_core, partner, rowpad),
            jnp.where(first_core, precv, recv),
        ],
        axis=0,
    )
    nf, nr = 2 * fd + 2, rd + 2
    nq = 2 * fd
    qtok = padded[1 : nf - 1, 1 : nr - 1].reshape(-1, dim)
    ptok = padded.reshape(-1, dim)

    span = 9 * ncols
    kidx = jnp.arange(span, dtype=jnp.int32)
    dframe = kidx // (3 * ncols) - 1
    drow = kidx // ncols % 3 - 1
    kcol = kidx % ncols
    qcol = jnp.arange(ncols, dtype=jnp.int32)
    coldist = jnp.abs(qcol[:, None] // TILE_W - kcol[None, :] // TILE_W)
    line = jnp.arange(nq * rd, dtype=jnp.int32)
    gframe = tp * nq + line // rd
    grow = h * rd + line % rd
    kf = gframe[:, None] + dframe[None, :]
    kr = grow[:, None] + drow[None, :]
    valid = (kf >= 0) & (kf < nt * fd) & (kr >= 0) & (kr < nh * rd)
    inv = 1.0 / HD**0.5

    def attend(wg, head0, hc):
        cw = hc * HD
        query = jnp.dot(qtok, wg[:, :cw], preferred_element_type=jnp.float32).astype(jnp.bfloat16)
        kv = jnp.dot(ptok, wg[:, cw:], preferred_element_type=jnp.float32).astype(jnp.bfloat16)
        keys = kv[:, :cw].reshape(nf, nr, ncols, hc, HD)
        values = kv[:, cw:].reshape(nf, nr, ncols, hc, HD)
        kwin = jnp.stack(
            [keys[f : f + 3, r : r + 3].reshape(span, hc, HD) for f in range(nq) for r in range(rd)]
        )
        vwin = jnp.stack(
            [values[f : f + 3, r : r + 3].reshape(span, hc, HD) for f in range(nq) for r in range(rd)]
        )
        qline = query.reshape(nq * rd, ncols, hc, HD)
        ext = lax.dynamic_slice_in_dim(extents, head0, hc, axis=0)
        allowed = valid[:, None, None, :] & (jnp.abs(dframe)[None, None, None, :] <= ext[None, :, 0, None, None])
        allowed = allowed & (jnp.abs(drow)[None, None, None, :] <= ext[None, :, 1, None, None])
        allowed = allowed & (coldist[None, None, :, :] <= ext[None, :, 2, None, None])
        scores = jnp.einsum("nqhd,nkhd->nhqk", qline, kwin, preferred_element_type=jnp.float32) * inv
        masked = jnp.where(allowed, scores, -1e30)
        top = jnp.max(masked, axis=-1, keepdims=True)
        expo = jnp.where(allowed, jnp.exp(masked - top), 0.0)
        weights = (expo / jnp.sum(expo, axis=-1, keepdims=True)).astype(jnp.bfloat16)
        out = jnp.einsum("nhqk,nkhd->nqhd", weights, vwin, preferred_element_type=jnp.float32)
        out = out.astype(jnp.bfloat16).reshape(nq, rd, ncols, cw)
        mine = lax.dynamic_slice_in_dim(out, c * fd, fd, axis=0)
        theirs = lax.dynamic_slice_in_dim(out, (1 - c) * fd, fd, axis=0)
        return mine, lax.ppermute(theirs, TM, swap)

    wsel = jnp.concatenate(
        [lax.dynamic_slice_in_dim(w_qkv, part * width + c * hw, hw, axis=1) for part in range(3)],
        axis=1,
    )
    wz = lax.all_gather(wsel, "hz", axis=0, tiled=True)
    outs = []
    first_head = 0
    for hc in CHUNKS:
        cw = hc * HD
        lo = first_head * HD
        wpart = jnp.concatenate([wz[:, part * hw + lo : part * hw + lo + cw] for part in range(3)], axis=1)
        wg = lax.all_gather(wpart, "hx", axis=0, tiled=True)
        outs.append(attend(wg, c * hh + first_head, hc))
        first_head += hc
    mine = jnp.concatenate([o[0] for o in outs], axis=-1)
    got = jnp.concatenate([o[1] for o in outs], axis=-1)
    return jnp.where(
        first_core,
        jnp.concatenate([mine, got], axis=-1),
        jnp.concatenate([got, mine], axis=-1),
    )


def solution(mesh):
    nt, nh = mesh.shape["tm"], mesh.shape["height"]
    devs = np.asarray(mesh.devices).reshape(nt // 2, 2, nh // 4, 4)
    m = Mesh(devs, ("tp", "c", "hx", "hz"))
    in_specs = (P(TM, HT, None, None), P(), P(), P(HT, None), P())
    out_specs = P(TM, HT, None, None)
    return jax.shard_map(on_device, mesh=m, in_specs=in_specs, out_specs=out_specs, check_vma=False)
```

```python
import numpy as np
import functools

import jax
import jax.numpy as jnp
from jax import lax
from jax.experimental import pallas as pl
from jax.experimental.pallas import tpu as pltpu
from jax.sharding import Mesh, PartitionSpec as P


HW = 12
HD = 128
TILE_W = 8
CHUNKS = (4, 2)


def _attn_kernel(base_ref, ext_ref, q_ref, k_ref, v_ref, o_ref, s_ref, *, hc, rd, ncols, nframes, nrows, inv):
    n = pl.program_id(0)
    f = n // rd
    r = n % rd
    gf = base_ref[0] + f
    gr = base_ref[1] + r
    qi = lax.broadcasted_iota(jnp.int32, (ncols, ncols), 0) // TILE_W
    ki = lax.broadcasted_iota(jnp.int32, (ncols, ncols), 1) // TILE_W
    tdist = jnp.abs(qi - ki)
    for hh in range(hc):
        e0 = ext_ref[hh, 0]
        e1 = ext_ref[hh, 1]
        colok = tdist <= ext_ref[hh, 2]
        q = q_ref[hh, 0]
        top = jnp.full((ncols, 1), -1e30, jnp.float32)
        for a in range(3):
            for b in range(3):
                ok = (abs(a - 1) <= e0) & (abs(b - 1) <= e1)
                ok = ok & (gf + (a - 1) >= 0) & (gf + (a - 1) < nframes)
                ok = ok & (gr + (b - 1) >= 0) & (gr + (b - 1) < nrows)
                k = k_ref[hh, f + a, r + b]
                s = lax.dot_general(q, k, (((1,), (1,)), ((), ())), preferred_element_type=jnp.float32) * inv
                s = jnp.where(colok & ok, s, -1e30)
                s_ref[3 * a + b] = s
                top = jnp.maximum(top, jnp.max(s, axis=1, keepdims=True))
        tot = jnp.zeros((ncols, 1), jnp.float32)
        for i in range(9):
            a, b = divmod(i, 3)
            ok = (abs(a - 1) <= e0) & (abs(b - 1) <= e1)
            ok = ok & (gf + (a - 1) >= 0) & (gf + (a - 1) < nframes)
            ok = ok & (gr + (b - 1) >= 0) & (gr + (b - 1) < nrows)
            e = jnp.where(colok & ok, jnp.exp(s_ref[i] - top), 0.0)
            s_ref[i] = e
            tot = tot + jnp.sum(e, axis=1, keepdims=True)
        acc = jnp.zeros((ncols, HD), jnp.float32)
        for i in range(9):
            a, b = divmod(i, 3)
            w = (s_ref[i] / tot).astype(jnp.bfloat16)
            acc = acc + jnp.dot(w, v_ref[hh, f + a, r + b], preferred_element_type=jnp.float32)
        o_ref[hh, 0] = acc.astype(o_ref.dtype)


def window_attention(base, ext, q_h, k_h, v_h, *, rd, nframes, nrows):
    hc, nl, ncols, hd = q_h.shape
    _, nf, nr, _, _ = k_h.shape
    kern = functools.partial(_attn_kernel, hc=hc, rd=rd, ncols=ncols, nframes=nframes, nrows=nrows, inv=1.0 / HD**0.5)
    flops = 4 * nl * hc * ncols * 9 * ncols * hd
    nbytes = 2 * (q_h.size * 2 + k_h.size + v_h.size)
    return pl.pallas_call(
        kern,
        grid=(nl,),
        in_specs=[
            pl.BlockSpec(memory_space=pltpu.SMEM),
            pl.BlockSpec(memory_space=pltpu.SMEM),
            pl.BlockSpec((hc, 1, ncols, hd), lambda n: (0, n, 0, 0)),
            pl.BlockSpec((hc, nf, nr, ncols, hd), lambda n: (0, 0, 0, 0, 0)),
            pl.BlockSpec((hc, nf, nr, ncols, hd), lambda n: (0, 0, 0, 0, 0)),
        ],
        out_specs=pl.BlockSpec((hc, 1, ncols, hd), lambda n: (0, n, 0, 0)),
        out_shape=jax.ShapeDtypeStruct(q_h.shape, jnp.bfloat16),
        scratch_shapes=[pltpu.VMEM((9, ncols, ncols), jnp.float32)],
        cost_estimate=pl.CostEstimate(flops=flops, transcendentals=nl * hc * ncols * 9 * ncols, bytes_accessed=nbytes),
    )(base, ext, q_h, k_h, v_h)


TM = ("tp", "c")
HT = ("hx", "hz")


def on_device(latent, mod_shift, mod_scale, w_qkv, extents):
    fd, rd, ncols, dim = latent.shape
    nt = lax.axis_size("tp") * 2
    nh = lax.axis_size("hx") * lax.axis_size("hz")
    hh = HW // 2
    hw = hh * HD
    width = HW * HD
    c = lax.axis_index("c")
    tp = lax.axis_index("tp")
    h = lax.axis_index("hx") * lax.axis_size("hz") + lax.axis_index("hz")
    first_core = c == 0

    feats = latent.astype(jnp.float32)
    mean = jnp.mean(feats, axis=-1, keepdims=True)
    var = jnp.mean((feats - mean) ** 2, axis=-1, keepdims=True)
    normed = (feats - mean) * lax.rsqrt(var + 1e-06)
    mod = (normed * (1.0 + mod_scale) + mod_shift).astype(jnp.bfloat16)

    up = [(i, i + 1) for i in range(nh - 1)]
    down = [(i + 1, i) for i in range(nh - 1)]
    w_qkv, mod = lax.optimization_barrier((w_qkv, mod))
    before = lax.ppermute(mod[:, rd - 1 : rd], HT, up)
    after = lax.ppermute(mod[:, 0:1], HT, down)
    rowpad = jnp.concatenate([before, mod, after], axis=1)
    swap = [(i, i ^ 1) for i in range(nt)]
    partner = lax.ppermute(rowpad, TM, swap)
    edge = jnp.where(first_core, rowpad[0:1], rowpad[fd - 1 : fd])
    p1 = []
    for k in range(nt // 2):
        if 2 * k - 1 >= 0:
            p1.append((2 * k - 1, 2 * k))
        if 2 * k + 2 < nt:
            p1.append((2 * k + 2, 2 * k + 1))
    recv = lax.ppermute(edge, TM, p1)
    precv = lax.ppermute(recv, TM, swap)
    padded = jnp.concatenate(
        [
            jnp.where(first_core, recv, precv),
            jnp.where(first_core, rowpad, partner),
            jnp.where(first_core, partner, rowpad),
            jnp.where(first_core, precv, recv),
        ],
        axis=0,
    )
    nf, nr = 2 * fd + 2, rd + 2
    nq = 2 * fd
    qtok = padded[1 : nf - 1, 1 : nr - 1].reshape(-1, dim)
    ptok = padded.reshape(-1, dim)


    def attend(wg, head0, hc):
        cw = hc * HD
        query = jnp.dot(qtok, wg[:, :cw], preferred_element_type=jnp.float32).astype(jnp.bfloat16)
        kv = jnp.dot(ptok, wg[:, cw:], preferred_element_type=jnp.float32).astype(jnp.bfloat16)
        k_h = kv[:, :cw].reshape(nf, nr, ncols, hc, HD).transpose(3, 0, 1, 2, 4)
        v_h = kv[:, cw:].reshape(nf, nr, ncols, hc, HD).transpose(3, 0, 1, 2, 4)
        q_h = query.reshape(nq * rd, ncols, hc, HD).transpose(2, 0, 1, 3)
        ext = lax.dynamic_slice_in_dim(extents, head0, hc, axis=0)
        base = jnp.stack([tp * nq, h * rd]).astype(jnp.int32)
        out = window_attention(base, ext, q_h, k_h, v_h, rd=rd, nframes=nt * fd, nrows=nh * rd)
        out = out.transpose(1, 2, 0, 3).reshape(nq, rd, ncols, cw)
        mine = lax.dynamic_slice_in_dim(out, c * fd, fd, axis=0)
        theirs = lax.dynamic_slice_in_dim(out, (1 - c) * fd, fd, axis=0)
        return mine, lax.ppermute(theirs, TM, swap)

    wsel = jnp.concatenate(
        [lax.dynamic_slice_in_dim(w_qkv, part * width + c * hw, hw, axis=1) for part in range(3)],
        axis=1,
    )
    wz = lax.all_gather(wsel, "hz", axis=0, tiled=True)
    outs = []
    first_head = 0
    for hc in CHUNKS:
        cw = hc * HD
        lo = first_head * HD
        wpart = jnp.concatenate([wz[:, part * hw + lo : part * hw + lo + cw] for part in range(3)], axis=1)
        wg = lax.all_gather(wpart, "hx", axis=0, tiled=True)
        outs.append(attend(wg, c * hh + first_head, hc))
        first_head += hc
    mine = jnp.concatenate([o[0] for o in outs], axis=-1)
    got = jnp.concatenate([o[1] for o in outs], axis=-1)
    return jnp.where(
        first_core,
        jnp.concatenate([mine, got], axis=-1),
        jnp.concatenate([got, mine], axis=-1),
    )


def solution(mesh):
    nt, nh = mesh.shape["tm"], mesh.shape["height"]
    devs = np.asarray(mesh.devices).reshape(nt // 2, 2, nh // 4, 4)
    m = Mesh(devs, ("tp", "c", "hx", "hz"))
    in_specs = (P(TM, HT, None, None), P(), P(), P(HT, None), P())
    out_specs = P(TM, HT, None, None)
    return jax.shard_map(on_device, mesh=m, in_specs=in_specs, out_specs=out_specs, check_vma=False)
```
